32 devices in a mesh: slot: 2 (over x), tile: 4 (over z), obs: 4 (over y, core).
Axes of the slice: x: 2, y: 2, z: 4, core: 2. Of those that a mesh axis runs over, the one named last changes fastest.
Arguments:
- forcing: float32 [2, 128, 32, 512], P('slot', None, 'tile', 'obs'), may hold values from -6 to 6
- winds: float32 [2, 2, 32, 512], P(None, 'slot', 'tile', 'obs'), may hold values from -0.2 to 0.2
- mixing: float32 [128, 128], replicated, may hold values from -0.12 to 0.12
- observation_columns: int32 [4, 2, 8192], P(None, 'slot', ('tile', 'obs')), may hold values from 0 to 1023
- obs_weights: float32 [4, 2, 8192], P(None, 'slot', ('tile', 'obs')), may hold values from 0.05 to 0.5
- obs_counts: int32 [2, 16, 4], P('slot', ('tile', 'obs')), may hold values from 16 to 128, as said below
- jacobian: float32 [2, 4, 128, 128], P('slot', 'obs'), may hold values from -0.5 to 0.5
Outputs:
- states: float32 [2, 128, 32, 512], P('slot', None, 'tile', 'obs')
- radiances: float32 [2, 128, 8192], P('slot', None, ('tile', 'obs'))
The draws below stay inside these ranges and needn't reach their ends.
Inputs may be any that keep to these rules, and one draw needn't show every extreme that they name: `obs_counts`: every block of 128 rows has its live rows first; in every slot and every tile one owner's blocks are full from every source.
All inputs are finite; a program needn't handle non-finite values.
Results may differ from the reference program's by a relative error of at most 0.0001.
Values sent between devices are 32-bit elements; how exact they have to be, the bound alone decides.
A program may use at most 64 MiB of HBM per device.

```python
import jax
import jax.numpy as jnp
from jax import lax

VL = 128
CHAN = 128
STEPS = 4
CX = 8
CY = 128
CAP = 128
NX = 32
NY = 512
ROWS_ALL = 8192
N_SLOT = 2
N_TILE = 4
N_OBS = 4


def draw_obs_counts(key, part):
    lower = jax.random.randint(jax.random.fold_in(key, 11), (N_SLOT, N_TILE, N_OBS, N_OBS), CAP // 8, CAP // 2 + 1)
    chosen = jax.random.randint(jax.random.fold_in(key, 12), (N_SLOT, N_TILE, 1, 1), 0, N_OBS)
    owners = jnp.arange(N_OBS, dtype=jnp.int32).reshape(1, 1, 1, N_OBS)
    filled = jnp.where(owners == chosen, CAP, lower)
    return filled.reshape(N_SLOT, N_TILE * N_OBS, N_OBS).astype(jnp.int32)


def set_ends(values, own_key, low, largest):
    shape = values.shape
    place = [jax.random.randint(jax.random.fold_in(own_key, axis), (), 0, shape[axis]) for axis in range(len(shape))]
    values = values.at[tuple(place)].set(low)
    longest = shape.index(max(shape))
    place[longest] = (place[longest] + 1) % shape[longest]
    return values.at[tuple(place)].set(largest)


def steps_of(rng, shape, shards, smallest, largest):
    def one(dim, blocks):
        draws = jax.random.uniform(jax.random.fold_in(jax.random.fold_in(rng, 6), dim), (blocks,), jnp.float32, smallest / len(shards), largest / len(shards))
        return jnp.repeat(jnp.exp(draws), shape[dim] // blocks).reshape((-1,) + (1,) * (len(shape) - dim - 1))

    gain = one(*shards[0])
    for cut in shards[1:]:
        gain = gain * one(*cut)
    return gain


def noise(own_key, extent, scale, bound, cuts=(), held_as=jnp.bfloat16):
    values = scale * jax.random.normal(own_key, extent, jnp.float32)
    if cuts:
        values = values * steps_of(own_key, extent, cuts, -0.22, 0.18)
    return jnp.clip(values, -bound, bound).astype(held_as)


def setup_inputs(seed: int = 0) -> dict:
    splits = jax.random.split(jax.random.key(seed), 8)
    forcing = noise(splits[0], (N_SLOT, VL, NX, NY), 1.0, 6.0, ((0, 2), (2, 4), (3, 4)), jnp.float32)
    winds = jnp.clip(jax.random.uniform(splits[1], (2, N_SLOT, NX, NY), jnp.float32, -0.2, 0.2) * steps_of(splits[1], (2, N_SLOT, NX, NY), ((1, 2), (2, 4), (3, 4)), -0.4, 0.0), -0.2, 0.2)
    mixing = noise(splits[2], (VL, VL), 0.02, 0.12, (), jnp.float32)
    observation_columns = set_ends(jax.random.randint(splits[3], (4, N_SLOT, ROWS_ALL), 0, CX * CY), jax.random.fold_in(splits[3], 1), 0, (CX * CY) - 1).astype(jnp.int32)
    obs_weights = jnp.clip(0.05 + 0.45 * jax.random.uniform(splits[4], (4, N_SLOT, ROWS_ALL), jnp.float32) ** steps_of(splits[4], (4, N_SLOT, ROWS_ALL), ((1, 2), (2, 16)), -0.2, 0.2), 0.05, 0.5)
    obs_counts = draw_obs_counts(jax.random.fold_in(splits[7], 71), 0)
    jacobian = noise(splits[6], (N_SLOT, N_OBS, CHAN, VL), VL ** -0.5, 0.5, ((0, 2), (1, 4)), jnp.float32)
    return dict(forcing=forcing, winds=winds, mixing=mixing, observation_columns=observation_columns, obs_weights=obs_weights, obs_counts=obs_counts, jacobian=jacobian)


mixing_rate = 0.15


def advance_slot(padded, eastward_rate, northward_rate, mixing):
    centre = padded[:, 1:-1, 1:-1]
    eastern = padded[:, 2:, 1:-1]
    western = padded[:, :-2, 1:-1]
    northern = padded[:, 1:-1, 2:]
    southern = padded[:, 1:-1, :-2]
    shifted_state = centre + eastward_rate * (eastern - western) + northward_rate * (northern - southern)
    shifted_state = shifted_state + mixing_rate * (eastern + western + northern + southern - 4.0 * centre)
    return shifted_state + jnp.einsum("mn,nlk->mlk", mixing, shifted_state, precision=lax.Precision.HIGHEST)


def reference(forcing, winds, mixing, observation_columns, obs_weights, obs_counts, jacobian):
    states = [forcing[0]]
    for slot_index in range(1, N_SLOT):
        current = states[-1]
        for step in range(STEPS):
            padded = jnp.pad(current, ((0, 0), (1, 1), (1, 1)), mode="wrap")
            current = advance_slot(padded, winds[0, slot_index - 1], winds[1, slot_index - 1], mixing)
        states.append(current + forcing[slot_index])
    owner_blocks = N_TILE * N_OBS
    rows = N_OBS * CAP
    columns = CX * CY
    radiances = []
    for slot_index in range(N_SLOT):
        patch = states[slot_index].reshape(VL, N_TILE, CX, N_OBS, CY).transpose(1, 3, 0, 2, 4).reshape(owner_blocks, VL, columns)
        cells = observation_columns[:, slot_index].reshape(4, owner_blocks, rows)
        weights = obs_weights[:, slot_index].reshape(4, owner_blocks, rows)
        profile = jnp.zeros((owner_blocks, VL, rows), jnp.float32)
        for corner in range(4):
            index = jnp.broadcast_to(cells[corner][:, None, :], (owner_blocks, VL, rows)).astype(jnp.int32)
            picked = jnp.take_along_axis(patch, index, axis=2)
            profile = profile + weights[corner][:, None, :] * picked
        live = (jnp.arange(CAP, dtype=jnp.int32).reshape(1, 1, CAP) < obs_counts[slot_index][:, :, None]).astype(jnp.float32)
        profile = profile.reshape(N_TILE, N_OBS, VL, N_OBS, CAP) * live.reshape(N_TILE, N_OBS, 1, N_OBS, CAP)
        slot_output = jnp.einsum("ocv,tsvok->tocsk", jacobian[slot_index], profile, precision=lax.Precision.HIGHEST)
        radiances.append(slot_output.transpose(2, 0, 1, 3, 4).reshape(CHAN, owner_blocks * rows))
    return jnp.stack(states), jnp.stack(radiances)
```

```python
import functools

import jax
import jax.numpy as jnp
from jax import lax
from jax.experimental import pallas as pl
from jax.experimental.pallas import tpu as pltpu
from jax.sharding import PartitionSpec as P

STEPS = 4
mixing_rate = 0.15
MESH = pl.DeviceIdType.MESH
SUB = 8
LANES = 128

TILE_DIRS = ((1, 0), (-1, 0))
EDGE_DIRS = ((0, 1), (0, -1), (1, 1), (1, -1), (-1, 1), (-1, -1))
DIRS = TILE_DIRS + EDGE_DIRS


def halves(x):
    high = x.astype(jnp.bfloat16)
    return high, (x - high.astype(jnp.float32)).astype(jnp.bfloat16)


def dot(a, b):
    return jnp.dot(a, b, preferred_element_type=jnp.float32)


def dot3(a, b):
    return dot(a[0], b[0]) + (dot(a[0], b[1]) + dot(a[1], b[0]))


def exact(a, b):
    return jnp.dot(a, b, precision=lax.Precision.HIGHEST, preferred_element_type=jnp.float32)


def kernel(
    n_slot, n_tile, n_obs,
    f_ref, winds_ref, mixing_ref, cells_ref, weights_ref, counts_ref, jac_ref,
    state_ref, rad_ref,
    ft, halo, packed, edges, rates, coef, gs, gr, w_hi, w_lo, pf, rf, pg, rg,
    halo_send, halo_recv, edge_send, edge_recv, rate_send, rate_recv,
    g_send, g_recv, pf_send, pf_recv, pg_send, pg_recv,
):
    slot = lax.axis_index("slot")
    tile = lax.axis_index("tile")
    obs = lax.axis_index("obs")
    cx, levels, cy = ft.shape
    rows = cells_ref.shape[1]
    cap = rows // n_obs
    span = cx * 2 * STEPS
    groups = LANES // span
    depth = SUB * groups
    chunks = levels // depth

    def neighbour(dt, do):
        return {"slot": slot, "tile": lax.rem(tile + dt + n_tile, n_tile), "obs": lax.rem(obs + do + n_obs, n_obs)}

    def peer(by):
        return {"slot": slot, "tile": tile, "obs": lax.rem(obs + by, n_obs)}

    def along(by):
        return {"slot": lax.rem(slot + by + n_slot, n_slot), "tile": tile, "obs": obs}

    def remote(src, dst, send, recv, to):
        return pltpu.make_async_remote_copy(
            src_ref=src, dst_ref=dst, send_sem=send, recv_sem=recv, device_id=to, device_id_type=MESH
        )

    def part(c):
        return pl.ds(pl.multiple_of(c * depth, depth), depth)

    def halo_copy(k, c):
        first = cx - STEPS if k == 0 else 0
        return remote(
            ft.at[pl.ds(first, STEPS), part(c), :], halo.at[k, :, part(c), :],
            halo_send.at[k, c], halo_recv.at[k, c], neighbour(*TILE_DIRS[k]),
        )

    def edge_copy(k, c):
        return remote(
            packed.at[c], edges.at[k, c], edge_send.at[k, c], edge_recv.at[k, c], neighbour(*EDGE_DIRS[k])
        )

    def rate_copy(k):
        return remote(winds_ref, rates.at[k], rate_send.at[k], rate_recv.at[k], neighbour(*DIRS[k]))

    def g_copy(c):
        return remote(
            gs.at[:, part(c), :], gr.at[:, part(c), :], g_send.at[c], g_recv.at[c], along(1)
        )

    def pf_copy(by):
        return remote(
            pf.at[lax.rem(obs + by, n_obs)], rf.at[obs], pf_send.at[by], pf_recv.at[by], peer(by)
        )

    def pg_copy(by, c):
        return remote(
            pg.at[lax.rem(obs + by, n_obs), part(c), :], rg.at[obs, part(c), :],
            pg_send.at[by, c], pg_recv.at[by, c], peer(by),
        )

    def each_chunk(body):
        def step(c, carry):
            body(c)
            return carry

        lax.fori_loop(0, chunks, step, 0)

    lane = lax.broadcasted_iota(jnp.int32, (SUB, LANES), 1)

    def pack(src):
        def one(c):
            out = jnp.zeros((SUB, LANES), jnp.float32)
            for h in range(groups):
                for x in range(cx):
                    level = pl.multiple_of(c * depth + h * SUB, SUB)
                    v = src[pl.ds(level * cx + x, SUB, stride=cx), :]
                    ft[x, pl.ds(level, SUB), :] = v
                    low = h * span + x * 2 * STEPS
                    moved = pltpu.roll(v, (low + STEPS) % LANES, 1)
                    out = jnp.where((lane >= low) & (lane < low + 2 * STEPS), moved, out)
            packed[c] = out

        each_chunk(one)

    def send_halos():
        def one(c):
            for k in range(len(TILE_DIRS)):
                halo_copy(k, c).start()
            for k in range(len(EDGE_DIRS)):
                edge_copy(k, c).start()

        each_chunk(one)

    def source_of(x):
        if x < 0:
            return 1, x + cx
        if x >= cx:
            return -1, x - cx
        return 0, x

    def forward():
        for k in range(len(DIRS)):
            rate_copy(k).wait_recv()
        for x in range(1 - STEPS, cx + STEPS - 1):
            dt, row = source_of(x)
            for which in range(2):
                def spread(ref):
                    return jnp.broadcast_to(ref[which, pl.ds(row, 1), :], (SUB, LANES))

                main = spread(winds_ref) if dt == 0 else spread(rates.at[DIRS.index((dt, 0))])
                west = spread(rates.at[DIRS.index((dt, 1))])
                east = spread(rates.at[DIRS.index((dt, -1))])
                side = jnp.where(lane < LANES // 2, east, west)
                for place, rate in ((0, main), (1, side)):
                    coef[x + STEPS, place, 2 * which] = mixing_rate + rate
                    coef[x + STEPS, place, 2 * which + 1] = mixing_rate - rate

        first_lane = lane == 0
        last_lane = lane == LANES - 1
        lower = lax.rem(lane, 2 * STEPS) < STEPS

        def one(c):
            for k in range(len(TILE_DIRS)):
                halo_copy(k, c).wait_recv()
            for k in range(len(EDGE_DIRS)):
                edge_copy(k, c).wait_recv()

            def group(h, carry):
                level = pl.ds(pl.multiple_of(c * depth + h * SUB, SUB), SUB)
                joined = {
                    dt: jnp.where(lower, edges[EDGE_DIRS.index((dt, 1)), c], edges[EDGE_DIRS.index((dt, -1)), c])
                    for dt in (-1, 0, 1)
                }
                joined = {dt: pltpu.roll(v, LANES - h * span, 1) for dt, v in joined.items()}
                main, side = {}, {}
                for x in range(-STEPS, cx + STEPS):
                    dt, row = source_of(x)
                    if dt == 0:
                        main[x] = ft[row, level, :]
                    elif dt == 1:
                        main[x] = halo[0, row - (cx - STEPS), level, :]
                    else:
                        main[x] = halo[1, row, level, :]
                    side[x] = pltpu.roll(joined[dt], (-(row * 2 * STEPS + STEPS)) % LANES, 1)
                for step in range(STEPS):
                    new_main, new_side = {}, {}
                    for x in range(step + 1 - STEPS, cx + STEPS - 1 - step):
                        m, e = main[x], side[x]
                        m_up, e_up = pltpu.roll(m, 1, 1), pltpu.roll(e, 1, 1)
                        m_down, e_down = pltpu.roll(m, LANES - 1, 1), pltpu.roll(e, LANES - 1, 1)

                        def mixed(place, centre, east, west, north, south):
                            k = x + STEPS
                            return (
                                (1.0 - 4.0 * mixing_rate) * centre
                                + (coef[k, place, 0] * east + coef[k, place, 1] * west)
                                + (coef[k, place, 2] * north + coef[k, place, 3] * south)
                            )

                        new_main[x] = mixed(
                            0, m, main[x + 1], main[x - 1],
                            jnp.where(last_lane, e_down, m_down), jnp.where(first_lane, e_up, m_up),
                        )
                        if step < STEPS - 1:
                            new_side[x] = mixed(
                                1, e, side[x + 1], side[x - 1],
                                jnp.where(last_lane, m_down, e_down), jnp.where(first_lane, m_up, e_up),
                            )
                    main, side = new_main, new_side
                for x in range(cx):
                    gs[x, level, :] = main[x]
                return carry

            lax.fori_loop(0, groups, group, 0)
            g_copy(c).start()

        each_chunk(one)

    barrier = pltpu.get_barrier_semaphore()
    greeted = [neighbour(*d) for d in DIRS] + [peer(by) for by in range(1, n_obs)] + [along(1), along(-1)]
    for to in greeted:
        pl.semaphore_signal(barrier, inc=1, device_id=to, device_id_type=MESH)

    @pl.when(slot == 0)
    def _():
        pack(f_ref)

    pl.semaphore_wait(barrier, len(greeted))

    @pl.when(slot < n_slot - 1)
    def _():
        for k in range(len(DIRS)):
            rate_copy(k).start()

    @pl.when(slot == 0)
    def _():
        send_halos()
        forward()

    tall = cy
    base = lax.broadcasted_iota(jnp.int32, (tall, cap), 0)
    live_row = lax.broadcasted_iota(jnp.int32, (1, cap), 1)

    def owner_weights(q, carry):
        cols = pl.ds(pl.multiple_of(q * cap, cap), cap)
        live = live_row < counts_ref[0, q]
        cell = [cells_ref[pl.ds(p, 1), cols] for p in range(cells_ref.shape[0])]
        weight = [jnp.where(live, weights_ref[pl.ds(p, 1), cols], 0.0) for p in range(cells_ref.shape[0])]

        def row_weights(x, inner):
            total = jnp.zeros((tall, cap), jnp.float32)
            for p in range(len(cell)):
                total = total + jnp.where(base == cell[p] - x * tall, weight[p], 0.0)
            high, low = halves(total)
            at = pl.ds(pl.multiple_of(x * tall, tall), tall)
            w_hi[at, cols] = high
            w_lo[at, cols] = low
            return inner

        lax.fori_loop(0, cx, row_weights, 0)
        return carry

    lax.fori_loop(0, n_obs, owner_weights, 0)

    wide = 2 * cap if n_obs % 2 == 0 else cap

    def interpolate(pieces, keep):
        parts = [halves(v) for v in pieces]
        high = jnp.concatenate([p[0] for p in parts], axis=1)
        low = jnp.concatenate([p[1] for p in parts], axis=1)
        both = jnp.concatenate([high, low], axis=0)
        tall_in = high.shape[0]

        def one(b, carry):
            cols = pl.ds(pl.multiple_of(b * wide, wide), wide)
            main = dot(both, w_hi[:, cols])
            total = main[:tall_in] + (main[tall_in:] + dot(high, w_lo[:, cols]))
            for j in range(wide // cap):
                keep(b * (wide // cap) + j, total[:, j * cap : (j + 1) * cap])
            return carry

        lax.fori_loop(0, rows // wide, one, 0)

    def keep_pf(q, value):
        pf[q] = value

    interpolate([f_ref[pl.ds(x, levels, stride=cx), :] for x in range(cx)], keep_pf)
    for by in range(1, n_obs):
        pf_copy(by).start()

    eye = jnp.where(
        lax.broadcasted_iota(jnp.int32, (levels, levels), 0) == lax.broadcasted_iota(jnp.int32, (levels, levels), 1),
        1.0, 0.0,
    )
    power = eye + mixing_ref[...]
    for _ in range(STEPS.bit_length() - 1):
        power = exact(power, power)
    jac = jac_ref[...]

    @pl.when(slot > 0)
    def _():
        def one(c):
            g_copy(c).wait_recv()

            def keep_pg(q, value):
                pg[q, part(c), :] = value

            interpolate([gr[x, part(c), :] for x in range(cx)], keep_pg)
            for by in range(1, n_obs):
                pg_copy(by, c).start()

        each_chunk(one)
        power_parts = halves(power)

        for x in range(cx):
            state = dot3(power_parts, halves(gr[x])) + f_ref[pl.ds(x, levels, stride=cx), :]
            state_ref[pl.ds(x, levels, stride=cx), :] = state

    @pl.when(slot == 0)
    def _():
        state_ref[...] = f_ref[...]

    if n_slot > 2:
        @pl.when((slot > 0) & (slot < n_slot - 1))
        def _():
            pack(state_ref)
            send_halos()
            forward()

    def owner_out(o, value):
        rad_ref[:, pl.ds(pl.multiple_of(o * cap, cap), cap)] = value

    rf[obs] = pf[obs]
    for by in range(1, n_obs):
        pf_copy(by).wait_recv()

    @pl.when(slot > 0)
    def _():
        rg[obs] = pg[obs]

        def arrived(c):
            for by in range(1, n_obs):
                pg_copy(by, c).wait_recv()

        each_chunk(arrived)
        table = halves(jnp.concatenate([jac, exact(jac, power)], axis=1))

        def one(o, carry):
            owner_out(o, dot3(table, halves(jnp.concatenate([rf[o], rg[o]], axis=0))))
            return carry

        lax.fori_loop(0, n_obs, one, 0)

    @pl.when(slot == 0)
    def _():
        table = halves(jac)

        def one(o, carry):
            owner_out(o, dot3(table, halves(rf[o])))
            return carry

        lax.fori_loop(0, n_obs, one, 0)

    for by in range(1, n_obs):
        pf_copy(by).wait_send()

    @pl.when(slot > 0)
    def _():
        def left(c):
            for by in range(1, n_obs):
                pg_copy(by, c).wait_send()

        each_chunk(left)

    @pl.when(slot < n_slot - 1)
    def _():
        for k in range(len(DIRS)):
            rate_copy(k).wait_send()

        def left(c):
            for k in range(len(TILE_DIRS)):
                halo_copy(k, c).wait_send()
            for k in range(len(EDGE_DIRS)):
                edge_copy(k, c).wait_send()
            g_copy(c).wait_send()

        each_chunk(left)


def solution(mesh):
    n_slot, n_tile, n_obs = (mesh.shape[a] for a in ("slot", "tile", "obs"))

    def local(forcing, winds, mixing, observation_columns, obs_weights, obs_counts, jacobian):
        _, levels, cx, cy = forcing.shape
        rows = observation_columns.shape[2]
        cap = rows // n_obs
        channels = jacobian.shape[2]
        chunks = levels // (SUB * (LANES // (cx * 2 * STEPS)))
        f32, bf16 = jnp.float32, jnp.bfloat16
        dma = pltpu.SemaphoreType.DMA
        vmem = pl.BlockSpec(memory_space=pltpu.VMEM)
        states, radiances = pl.pallas_call(
            functools.partial(kernel, n_slot, n_tile, n_obs),
            out_shape=(
                jax.ShapeDtypeStruct((levels * cx, cy), f32),
                jax.ShapeDtypeStruct((channels, rows), f32),
            ),
            in_specs=[vmem] * 5 + [pl.BlockSpec(memory_space=pltpu.SMEM), vmem],
            out_specs=(vmem, vmem),
            scratch_shapes=[
                pltpu.VMEM((cx, levels, cy), f32),
                pltpu.VMEM((2, STEPS, levels, cy), f32),
                pltpu.VMEM((chunks, SUB, LANES), f32),
                pltpu.VMEM((len(EDGE_DIRS), chunks, SUB, LANES), f32),
                pltpu.VMEM((len(DIRS), 2, cx, cy), f32),
                pltpu.VMEM((cx + 2 * STEPS, 2, 4, SUB, LANES), f32),
                pltpu.VMEM((cx, levels, cy), f32),
                pltpu.VMEM((cx, levels, cy), f32),
                pltpu.VMEM((cx * cy, rows), bf16),
                pltpu.VMEM((cx * cy, rows), bf16),
                pltpu.VMEM((n_obs, levels, cap), f32),
                pltpu.VMEM((n_obs, levels, cap), f32),
                pltpu.VMEM((n_obs, levels, cap), f32),
                pltpu.VMEM((n_obs, levels, cap), f32),
                dma((2, chunks)), dma((2, chunks)),
                dma((len(EDGE_DIRS), chunks)), dma((len(EDGE_DIRS), chunks)),
                dma((len(DIRS),)), dma((len(DIRS),)),
                dma((chunks,)), dma((chunks,)),
                dma((n_obs,)), dma((n_obs,)),
                dma((n_obs, chunks)), dma((n_obs, chunks)),
            ],
            compiler_params=pltpu.CompilerParams(
                collective_id=0, has_side_effects=True, vmem_limit_bytes=48 * 1024 * 1024
            ),
        )(
            forcing.reshape(levels * cx, cy),
            winds.reshape(2, cx, cy),
            mixing,
            observation_columns.reshape(-1, rows),
            obs_weights.reshape(-1, rows),
            obs_counts.reshape(1, n_obs),
            jacobian.reshape(channels, levels),
        )
        return states.reshape(1, levels, cx, cy), radiances.reshape(1, channels, rows)

    return jax.shard_map(
        local,
        mesh=mesh,
        in_specs=(
            P("slot", None, "tile", "obs"),
            P(None, "slot", "tile", "obs"),
            P(),
            P(None, "slot", ("tile", "obs")),
            P(None, "slot", ("tile", "obs")),
            P("slot", ("tile", "obs"), None),
            P("slot", "obs", None, None),
        ),
        out_specs=(P("slot", None, "tile", "obs"), P("slot", None, ("tile", "obs"))),
        check_vma=False,
    )
```

```python
import functools

import jax
import jax.numpy as jnp
from jax import lax
from jax.experimental import pallas as pl
from jax.experimental.pallas import tpu as pltpu
from jax.sharding import PartitionSpec as P

STEPS = 4
mixing_rate = 0.15
MESH = pl.DeviceIdType.MESH
SUB = 8
LANES = 128

TILE_DIRS = ((1, 0), (-1, 0))
EDGE_DIRS = ((0, 1), (0, -1), (1, 1), (1, -1), (-1, 1), (-1, -1))
DIRS = TILE_DIRS + EDGE_DIRS


def halves(x):
    high = x.astype(jnp.bfloat16)
    return high, (x - high.astype(jnp.float32)).astype(jnp.bfloat16)


def dot(a, b):
    return jnp.dot(a, b, preferred_element_type=jnp.float32)


def dot3(a, b):
    return dot(a[0], b[0]) + (dot(a[0], b[1]) + dot(a[1], b[0]))


def exact(a, b):
    return jnp.dot(a, b, precision=lax.Precision.HIGHEST, preferred_element_type=jnp.float32)


def kernel(
    n_slot, n_tile, n_obs,
    f_in, winds_in, mixing_in, cells_in, weights_in, counts_in, jac_in,
    state_ref, rad_ref,
    f_ref, winds_ref, mixing_ref, cells_ref, weights_ref, counts_ref, jac_ref, in_sem,
    ft, halo, packed, edges, rates, coef, gs, gr, w_hi, w_lo, pf, rf, pg, rg,
    halo_send, halo_recv, edge_send, edge_recv, rate_send, rate_recv,
    g_send, g_recv, pf_send, pf_recv, pg_send, pg_recv,
):
    slot = lax.axis_index("slot")
    tile = lax.axis_index("tile")
    obs = lax.axis_index("obs")
    cx, levels, cy = ft.shape
    rows = cells_ref.shape[2]
    cap = rows // n_obs
    span = cx * 2 * STEPS
    groups = LANES // span
    depth = SUB * groups
    chunks = levels // depth

    def neighbour(dt, do):
        return {"slot": slot, "tile": lax.rem(tile + dt + n_tile, n_tile), "obs": lax.rem(obs + do + n_obs, n_obs)}

    def peer(by):
        return {"slot": slot, "tile": tile, "obs": lax.rem(obs + by, n_obs)}

    def along(by):
        return {"slot": lax.rem(slot + by + n_slot, n_slot), "tile": tile, "obs": obs}

    def remote(src, dst, send, recv, to):
        return pltpu.make_async_remote_copy(
            src_ref=src, dst_ref=dst, send_sem=send, recv_sem=recv, device_id=to, device_id_type=MESH
        )

    def part(c):
        return pl.ds(pl.multiple_of(c * depth, depth), depth)

    def halo_copy(k, c):
        first = cx - STEPS if k == 0 else 0
        return remote(
            ft.at[pl.ds(first, STEPS), part(c), :], halo.at[k, :, part(c), :],
            halo_send.at[k, c], halo_recv.at[k, c], neighbour(*TILE_DIRS[k]),
        )

    edge_parts = (pl.ds(0, 1), pl.ds(1, chunks - 1))

    def edge_copy(k, i):
        return remote(
            packed.at[edge_parts[i]], edges.at[k, edge_parts[i]],
            edge_send.at[k, i], edge_recv.at[k, i], neighbour(*EDGE_DIRS[k]),
        )

    def rate_copy(k):
        return remote(winds_ref, rates.at[k], rate_send.at[k], rate_recv.at[k], neighbour(*DIRS[k]))

    def g_copy(c):
        return remote(
            gs.at[:, part(c), :], gr.at[:, part(c), :], g_send.at[c], g_recv.at[c], along(1)
        )

    def pf_copy(by):
        return remote(
            pf.at[lax.rem(obs + by, n_obs)], rf.at[obs], pf_send.at[by], pf_recv.at[by], peer(by)
        )

    def pg_copy(by, c):
        return remote(
            pg.at[lax.rem(obs + by, n_obs), part(c), :], rg.at[obs, part(c), :],
            pg_send.at[by, c], pg_recv.at[by, c], peer(by),
        )

    def each_chunk(body, first=0, last=chunks):
        def step(c, carry):
            body(c)
            return carry

        lax.fori_loop(first, last, step, 0)

    lane = lax.broadcasted_iota(jnp.int32, (SUB, LANES), 1)

    def pack(src):
        def one(c):
            out = jnp.zeros((SUB, LANES), jnp.float32)
            for h in range(groups):
                for x in range(cx):
                    level = pl.multiple_of(c * depth + h * SUB, SUB)
                    v = src[pl.ds(level * cx + x, SUB, stride=cx), :]
                    ft[x, pl.ds(level, SUB), :] = v
                    low = h * span + x * 2 * STEPS
                    moved = pltpu.roll(v, (low + STEPS) % LANES, 1)
                    out = jnp.where((lane >= low) & (lane < low + 2 * STEPS), moved, out)
            packed[c] = out

        each_chunk(one)

    def send_halos():
        def one(c):
            for k in range(len(TILE_DIRS)):
                halo_copy(k, c).start()

        for i, first in enumerate((0, 1)):
            for k in range(len(EDGE_DIRS)):
                edge_copy(k, i).start()
            each_chunk(one, first, chunks if i else 1)

    def source_of(x):
        if x < 0:
            return 1, x + cx
        if x >= cx:
            return -1, x - cx
        return 0, x

    def build_coefs():
        for k in range(len(DIRS)):
            rate_copy(k).wait_recv()
        for x in range(1 - STEPS, cx + STEPS - 1):
            dt, row = source_of(x)
            for which in range(2):
                def spread(ref):
                    return jnp.broadcast_to(ref[which, pl.ds(row, 1), :], (SUB, LANES))

                main = spread(winds_ref) if dt == 0 else spread(rates.at[DIRS.index((dt, 0))])
                west = spread(rates.at[DIRS.index((dt, 1))])
                east = spread(rates.at[DIRS.index((dt, -1))])
                side = jnp.where(lane < LANES // 2, east, west)
                for place, rate in ((0, main), (1, side)):
                    coef[x + STEPS, place, 2 * which] = mixing_rate + rate
                    coef[x + STEPS, place, 2 * which + 1] = mixing_rate - rate

    def forward(first, last):
        first_lane = lane == 0
        last_lane = lane == LANES - 1
        lower = lax.rem(lane, 2 * STEPS) < STEPS

        def one(c):
            for k in range(len(TILE_DIRS)):
                halo_copy(k, c).wait_recv()

            def group(h, carry):
                level = pl.ds(pl.multiple_of(c * depth + h * SUB, SUB), SUB)
                joined = {
                    dt: jnp.where(lower, edges[EDGE_DIRS.index((dt, 1)), c], edges[EDGE_DIRS.index((dt, -1)), c])
                    for dt in (-1, 0, 1)
                }
                joined = {dt: pltpu.roll(v, LANES - h * span, 1) for dt, v in joined.items()}
                main, side = {}, {}
                for x in range(-STEPS, cx + STEPS):
                    dt, row = source_of(x)
                    if dt == 0:
                        main[x] = ft[row, level, :]
                    elif dt == 1:
                        main[x] = halo[0, row - (cx - STEPS), level, :]
                    else:
                        main[x] = halo[1, row, level, :]
                    side[x] = pltpu.roll(joined[dt], (-(row * 2 * STEPS + STEPS)) % LANES, 1)
                for step in range(STEPS):
                    new_main, new_side = {}, {}
                    for x in range(step + 1 - STEPS, cx + STEPS - 1 - step):
                        m, e = main[x], side[x]
                        m_up, e_up = pltpu.roll(m, 1, 1), pltpu.roll(e, 1, 1)
                        m_down, e_down = pltpu.roll(m, LANES - 1, 1), pltpu.roll(e, LANES - 1, 1)

                        def mixed(place, centre, east, west, north, south):
                            k = x + STEPS
                            return (
                                (1.0 - 4.0 * mixing_rate) * centre
                                + (coef[k, place, 0] * east + coef[k, place, 1] * west)
                                + (coef[k, place, 2] * north + coef[k, place, 3] * south)
                            )

                        new_main[x] = mixed(
                            0, m, main[x + 1], main[x - 1],
                            jnp.where(last_lane, e_down, m_down), jnp.where(first_lane, e_up, m_up),
                        )
                        if step < STEPS - 1:
                            new_side[x] = mixed(
                                1, e, side[x + 1], side[x - 1],
                                jnp.where(last_lane, m_down, e_down), jnp.where(first_lane, m_up, e_up),
                            )
                    main, side = new_main, new_side
                for x in range(cx):
                    gs[x, level, :] = main[x]
                return carry

            lax.fori_loop(0, groups, group, 0)
            g_copy(c).start()

        if first < 2:
            for k in range(len(EDGE_DIRS)):
                edge_copy(k, first).wait_recv()
        each_chunk(one, first, last)

    tall = cy
    base = lax.broadcasted_iota(jnp.int32, (tall, cap), 0)
    live_row = lax.broadcasted_iota(jnp.int32, (1, cap), 1)

    def owner_weights(q, carry):
        cols = pl.ds(pl.multiple_of(q * cap, cap), cap)
        live = live_row < counts_ref[0, 0, q]
        cell = [cells_ref[p, :, cols] for p in range(cells_ref.shape[0])]
        weight = [jnp.where(live, weights_ref[p, :, cols], 0.0) for p in range(cells_ref.shape[0])]

        def row_weights(x, inner):
            total = jnp.zeros((tall, cap), jnp.float32)
            for p in range(len(cell)):
                total = total + jnp.where(base == cell[p] - x * tall, weight[p], 0.0)
            high, low = halves(total)
            at = pl.ds(pl.multiple_of(x * tall, tall), tall)
            w_hi[at, cols] = high
            w_lo[at, cols] = low
            return inner

        lax.fori_loop(0, cx, row_weights, 0)
        return carry


    wide = 2 * cap if n_obs % 2 == 0 else cap

    def interpolate(pieces, keep):
        parts = [halves(v) for v in pieces]
        high = jnp.concatenate([p[0] for p in parts], axis=1)
        low = jnp.concatenate([p[1] for p in parts], axis=1)
        both = jnp.concatenate([high, low], axis=0)
        tall_in = high.shape[0]

        def one(b, carry):
            cols = pl.ds(pl.multiple_of(b * wide, wide), wide)
            main = dot(both, w_hi[:, cols])
            total = main[:tall_in] + (main[tall_in:] + dot(high, w_lo[:, cols]))
            for j in range(wide // cap):
                keep(b * (wide // cap) + j, total[:, j * cap : (j + 1) * cap])
            return carry

        lax.fori_loop(0, rows // wide, one, 0)

    def keep_pf(q, value):
        pf[q] = value

    def interpolate_forcing():
        lax.fori_loop(0, n_obs, owner_weights, 0)
        interpolate([f_ref[pl.ds(x, levels, stride=cx), :] for x in range(cx)], keep_pf)

    early = chunks // 2

    barrier = pltpu.get_barrier_semaphore()
    greeted = [neighbour(*d) for d in DIRS] + [peer(by) for by in range(1, n_obs)] + [along(1), along(-1)]
    for to in greeted:
        pl.semaphore_signal(barrier, inc=1, device_id=to, device_id_type=MESH)

    pairs = (
        (winds_in, winds_ref), (f_in, f_ref), (cells_in, cells_ref), (weights_in, weights_ref),
        (counts_in, counts_ref), (mixing_in, mixing_ref), (jac_in, jac_ref),
    )
    fetches = [pltpu.make_async_copy(src, dst, in_sem.at[i]) for i, (src, dst) in enumerate(pairs)]
    for fetch in fetches:
        fetch.start()
    for fetch in fetches:
        fetch.wait()

    @pl.when(slot == 0)
    def _():
        pack(f_ref)

    @pl.when(slot > 0)
    def _():
        interpolate_forcing()

    pl.semaphore_wait(barrier, len(greeted))

    @pl.when(slot < n_slot - 1)
    def _():
        for k in range(len(DIRS)):
            rate_copy(k).start()

    @pl.when(slot == 0)
    def _():
        send_halos()
        build_coefs()
        forward(0, 1)
        forward(1, early)
        interpolate_forcing()

    for by in range(1, n_obs):
        pf_copy(by).start()

    @pl.when(slot == 0)
    def _():
        forward(early, chunks)

    eye = jnp.where(
        lax.broadcasted_iota(jnp.int32, (levels, levels), 0) == lax.broadcasted_iota(jnp.int32, (levels, levels), 1),
        1.0, 0.0,
    )
    power = eye + mixing_ref[...]
    for _ in range(STEPS.bit_length() - 1):
        power = exact(power, power)
    jac = jac_ref[...]

    @pl.when(slot > 0)
    def _():
        def one(c):
            g_copy(c).wait_recv()

            def keep_pg(q, value):
                pg[q, part(c), :] = value

            interpolate([gr[x, part(c), :] for x in range(cx)], keep_pg)
            for by in range(1, n_obs):
                pg_copy(by, c).start()

        each_chunk(one)
        power_parts = halves(power)

        for x in range(cx):
            state = dot3(power_parts, halves(gr[x])) + f_ref[pl.ds(x, levels, stride=cx), :]
            state_ref[pl.ds(x, levels, stride=cx), :] = state

    @pl.when(slot == 0)
    def _():
        state_ref[...] = f_ref[...]

    if n_slot > 2:
        @pl.when((slot > 0) & (slot < n_slot - 1))
        def _():
            pack(state_ref)
            send_halos()
            build_coefs()
            forward(0, 1)
            forward(1, early)
            forward(early, chunks)

    def owner_out(o, value):
        rad_ref[:, pl.ds(pl.multiple_of(o * cap, cap), cap)] = value

    rf[obs] = pf[obs]
    for by in range(1, n_obs):
        pf_copy(by).wait_recv()

    @pl.when(slot > 0)
    def _():
        rg[obs] = pg[obs]

        def arrived(c):
            for by in range(1, n_obs):
                pg_copy(by, c).wait_recv()

        each_chunk(arrived)
        table = halves(jnp.concatenate([jac, exact(jac, power)], axis=1))

        def one(o, carry):
            owner_out(o, dot3(table, halves(jnp.concatenate([rf[o], rg[o]], axis=0))))
            return carry

        lax.fori_loop(0, n_obs, one, 0)

    @pl.when(slot == 0)
    def _():
        table = halves(jac)

        def one(o, carry):
            owner_out(o, dot3(table, halves(rf[o])))
            return carry

        lax.fori_loop(0, n_obs, one, 0)

    for by in range(1, n_obs):
        pf_copy(by).wait_send()

    @pl.when(slot > 0)
    def _():
        def left(c):
            for by in range(1, n_obs):
                pg_copy(by, c).wait_send()

        each_chunk(left)

    @pl.when(slot < n_slot - 1)
    def _():
        for k in range(len(DIRS)):
            rate_copy(k).wait_send()

        def left(c):
            for k in range(len(TILE_DIRS)):
                halo_copy(k, c).wait_send()
            g_copy(c).wait_send()

        each_chunk(left)
        for k in range(len(EDGE_DIRS)):
            for i in range(2):
                edge_copy(k, i).wait_send()


def write_out(states, radiances, states_out, radiances_out, sem):
    copies = [
        pltpu.make_async_copy(states, states_out, sem.at[0]),
        pltpu.make_async_copy(radiances, radiances_out, sem.at[1]),
    ]
    for copy in copies:
        copy.start()
    for copy in copies:
        copy.wait()


def solution(mesh):
    n_slot, n_tile, n_obs = (mesh.shape[a] for a in ("slot", "tile", "obs"))

    def local(forcing, winds, mixing, observation_columns, obs_weights, obs_counts, jacobian):
        _, levels, cx, cy = forcing.shape
        rows = observation_columns.shape[2]
        cap = rows // n_obs
        channels = jacobian.shape[2]
        chunks = levels // (SUB * (LANES // (cx * 2 * STEPS)))
        f32, bf16 = jnp.float32, jnp.bfloat16
        dma = pltpu.SemaphoreType.DMA
        vmem = pl.BlockSpec(memory_space=pltpu.VMEM)
        hbm = pl.BlockSpec(memory_space=pltpu.HBM)
        states, radiances = pl.pallas_call(
            functools.partial(kernel, n_slot, n_tile, n_obs),
            out_shape=(
                jax.ShapeDtypeStruct((levels * cx, cy), f32),
                jax.ShapeDtypeStruct((channels, rows), f32),
            ),
            in_specs=[hbm] * 7,
            out_specs=(vmem, vmem),
            scratch_shapes=[
                pltpu.VMEM((levels * cx, cy), f32),
                pltpu.VMEM((2, cx, cy), f32),
                pltpu.VMEM(mixing.shape, f32),
                pltpu.VMEM(observation_columns.shape, jnp.int32),
                pltpu.VMEM(obs_weights.shape, f32),
                pltpu.SMEM(obs_counts.shape, jnp.int32),
                pltpu.VMEM((channels, levels), f32),
                dma((7,)),
                pltpu.VMEM((cx, levels, cy), f32),
                pltpu.VMEM((2, STEPS, levels, cy), f32),
                pltpu.VMEM((chunks, SUB, LANES), f32),
                pltpu.VMEM((len(EDGE_DIRS), chunks, SUB, LANES), f32),
                pltpu.VMEM((len(DIRS), 2, cx, cy), f32),
                pltpu.VMEM((cx + 2 * STEPS, 2, 4, SUB, LANES), f32),
                pltpu.VMEM((cx, levels, cy), f32),
                pltpu.VMEM((cx, levels, cy), f32),
                pltpu.VMEM((cx * cy, rows), bf16),
                pltpu.VMEM((cx * cy, rows), bf16),
                pltpu.VMEM((n_obs, levels, cap), f32),
                pltpu.VMEM((n_obs, levels, cap), f32),
                pltpu.VMEM((n_obs, levels, cap), f32),
                pltpu.VMEM((n_obs, levels, cap), f32),
                dma((2, chunks)), dma((2, chunks)),
                dma((len(EDGE_DIRS), 2)), dma((len(EDGE_DIRS), 2)),
                dma((len(DIRS),)), dma((len(DIRS),)),
                dma((chunks,)), dma((chunks,)),
                dma((n_obs,)), dma((n_obs,)),
                dma((n_obs, chunks)), dma((n_obs, chunks)),
            ],
            compiler_params=pltpu.CompilerParams(
                collective_id=0, has_side_effects=True, vmem_limit_bytes=48 * 1024 * 1024
            ),
        )(*(pltpu.with_memory_space_constraint(v, pltpu.HBM) for v in (
            forcing.reshape(levels * cx, cy),
            winds.reshape(2, cx, cy),
            mixing,
            observation_columns,
            obs_weights,
            obs_counts,
            jacobian.reshape(channels, levels),
        )))
        states, radiances = pl.pallas_call(
            write_out,
            out_shape=(
                jax.ShapeDtypeStruct((levels * cx, cy), f32),
                jax.ShapeDtypeStruct((channels, rows), f32),
            ),
            in_specs=[vmem, vmem],
            out_specs=(hbm, hbm),
            scratch_shapes=[dma((2,))],
            compiler_params=pltpu.CompilerParams(vmem_limit_bytes=2 * 1024 * 1024),
        )(states, radiances)
        return states.reshape(1, levels, cx, cy), radiances.reshape(1, channels, rows)

    return jax.shard_map(
        local,
        mesh=mesh,
        in_specs=(
            P("slot", None, "tile", "obs"),
            P(None, "slot", "tile", "obs"),
            P(),
            P(None, "slot", ("tile", "obs")),
            P(None, "slot", ("tile", "obs")),
            P("slot", ("tile", "obs"), None),
            P("slot", "obs", None, None),
        ),
        out_specs=(P("slot", None, "tile", "obs"), P("slot", None, ("tile", "obs"))),
        check_vma=False,
    )
```

```python
import functools

import jax
import jax.numpy as jnp
from jax import lax
from jax.experimental import pallas as pl
from jax.experimental.pallas import tpu as pltpu
from jax.sharding import PartitionSpec as P

STEPS = 4
mixing_rate = 0.15
MESH = pl.DeviceIdType.MESH
SUB = 8
LANES = 128

TILE_DIRS = ((1, 0), (-1, 0))
EDGE_DIRS = ((0, 1), (0, -1), (1, 1), (1, -1), (-1, 1), (-1, -1))
DIRS = TILE_DIRS + EDGE_DIRS


def halves(x):
    high = x.astype(jnp.bfloat16)
    return high, (x - high.astype(jnp.float32)).astype(jnp.bfloat16)


def dot(a, b):
    return jnp.dot(a, b, preferred_element_type=jnp.float32)


def dot3(a, b):
    return dot(a[0], b[0]) + (dot(a[0], b[1]) + dot(a[1], b[0]))


def exact(a, b):
    return jnp.dot(a, b, precision=lax.Precision.HIGHEST, preferred_element_type=jnp.float32)


def kernel(
    n_slot, n_tile, n_obs,
    f_in, winds_in, mixing_in, cells_in, weights_in, counts_in, jac_in,
    state_ref, rad_ref,
    f_ref, winds_ref, mixing_ref, cells_ref, weights_ref, counts_ref, jac_ref, in_sem, table_hi, table_lo,
    ft, halo, packed, edges, rates, coef, gs, gr, w_hi, w_lo, pf, rf, pg, rg,
    halo_send, halo_recv, edge_send, edge_recv, rate_send, rate_recv,
    g_send, g_recv, pf_send, pf_recv, pg_send, pg_recv,
):
    slot = lax.axis_index("slot")
    tile = lax.axis_index("tile")
    obs = lax.axis_index("obs")
    cx, levels, cy = ft.shape
    rows = cells_ref.shape[2]
    cap = rows // n_obs
    span = cx * 2 * STEPS
    groups = LANES // span
    depth = SUB * groups
    chunks = levels // depth

    def neighbour(dt, do):
        return {"slot": slot, "tile": lax.rem(tile + dt + n_tile, n_tile), "obs": lax.rem(obs + do + n_obs, n_obs)}

    def peer(by):
        return {"slot": slot, "tile": tile, "obs": lax.rem(obs + by, n_obs)}

    def along(by):
        return {"slot": lax.rem(slot + by + n_slot, n_slot), "tile": tile, "obs": obs}

    def remote(src, dst, send, recv, to):
        return pltpu.make_async_remote_copy(
            src_ref=src, dst_ref=dst, send_sem=send, recv_sem=recv, device_id=to, device_id_type=MESH
        )

    def part(c):
        return pl.ds(pl.multiple_of(c * depth, depth), depth)

    def halo_copy(k, c):
        first = cx - STEPS if k == 0 else 0
        return remote(
            ft.at[pl.ds(first, STEPS), part(c), :], halo.at[k, :, part(c), :],
            halo_send.at[k, c], halo_recv.at[k, c], neighbour(*TILE_DIRS[k]),
        )

    edge_parts = (pl.ds(0, 1), pl.ds(1, chunks - 1))

    def edge_copy(k, i):
        return remote(
            packed.at[edge_parts[i]], edges.at[k, edge_parts[i]],
            edge_send.at[k, i], edge_recv.at[k, i], neighbour(*EDGE_DIRS[k]),
        )

    def rate_copy(k):
        return remote(winds_ref, rates.at[k], rate_send.at[k], rate_recv.at[k], neighbour(*DIRS[k]))

    def g_copy(c):
        return remote(
            gs.at[:, part(c), :], gr.at[:, part(c), :], g_send.at[c], g_recv.at[c], along(1)
        )

    def pf_copy(by):
        return remote(
            pf.at[lax.rem(obs + by, n_obs)], rf.at[obs], pf_send.at[by], pf_recv.at[by], peer(by)
        )

    def pg_copy(by, c):
        return remote(
            pg.at[lax.rem(obs + by, n_obs), part(c), :], rg.at[obs, part(c), :],
            pg_send.at[by, c], pg_recv.at[by, c], peer(by),
        )

    def each_chunk(body, first=0, last=chunks):
        def step(c, carry):
            body(c)
            return carry

        lax.fori_loop(first, last, step, 0)

    lane = lax.broadcasted_iota(jnp.int32, (SUB, LANES), 1)

    def pack(src):
        def one(c):
            out = jnp.zeros((SUB, LANES), jnp.float32)
            for h in range(groups):
                for x in range(cx):
                    level = pl.multiple_of(c * depth + h * SUB, SUB)
                    v = src[pl.ds(level * cx + x, SUB, stride=cx), :]
                    ft[x, pl.ds(level, SUB), :] = v
                    low = h * span + x * 2 * STEPS
                    moved = pltpu.roll(v, (low + STEPS) % LANES, 1)
                    out = jnp.where((lane >= low) & (lane < low + 2 * STEPS), moved, out)
            packed[c] = out

        each_chunk(one)

    def send_halos():
        def one(c):
            for k in range(len(TILE_DIRS)):
                halo_copy(k, c).start()

        for i, first in enumerate((0, 1)):
            for k in range(len(EDGE_DIRS)):
                edge_copy(k, i).start()
            each_chunk(one, first, chunks if i else 1)

    def source_of(x):
        if x < 0:
            return 1, x + cx
        if x >= cx:
            return -1, x - cx
        return 0, x

    def build_coefs():
        for k in range(len(DIRS)):
            rate_copy(k).wait_recv()
        for x in range(1 - STEPS, cx + STEPS - 1):
            dt, row = source_of(x)
            for which in range(2):
                def spread(ref):
                    return jnp.broadcast_to(ref[which, pl.ds(row, 1), :], (SUB, LANES))

                main = spread(winds_ref) if dt == 0 else spread(rates.at[DIRS.index((dt, 0))])
                west = spread(rates.at[DIRS.index((dt, 1))])
                east = spread(rates.at[DIRS.index((dt, -1))])
                side = jnp.where(lane < LANES // 2, east, west)
                for place, rate in ((0, main), (1, side)):
                    coef[x + STEPS, place, 2 * which] = mixing_rate + rate
                    coef[x + STEPS, place, 2 * which + 1] = mixing_rate - rate

    def forward(first, last):
        first_lane = lane == 0
        last_lane = lane == LANES - 1
        lower = lax.rem(lane, 2 * STEPS) < STEPS

        def one(c):
            for k in range(len(TILE_DIRS)):
                halo_copy(k, c).wait_recv()

            def group(h, carry):
                level = pl.ds(pl.multiple_of(c * depth + h * SUB, SUB), SUB)
                joined = {
                    dt: jnp.where(lower, edges[EDGE_DIRS.index((dt, 1)), c], edges[EDGE_DIRS.index((dt, -1)), c])
                    for dt in (-1, 0, 1)
                }
                joined = {dt: pltpu.roll(v, LANES - h * span, 1) for dt, v in joined.items()}
                main, side = {}, {}
                for x in range(-STEPS, cx + STEPS):
                    dt, row = source_of(x)
                    if dt == 0:
                        main[x] = ft[row, level, :]
                    elif dt == 1:
                        main[x] = halo[0, row - (cx - STEPS), level, :]
                    else:
                        main[x] = halo[1, row, level, :]
                    side[x] = pltpu.roll(joined[dt], (-(row * 2 * STEPS + STEPS)) % LANES, 1)
                for step in range(STEPS):
                    new_main, new_side = {}, {}
                    for x in range(step + 1 - STEPS, cx + STEPS - 1 - step):
                        m, e = main[x], side[x]
                        m_up, e_up = pltpu.roll(m, 1, 1), pltpu.roll(e, 1, 1)
                        m_down, e_down = pltpu.roll(m, LANES - 1, 1), pltpu.roll(e, LANES - 1, 1)

                        def mixed(place, centre, east, west, north, south):
                            k = x + STEPS
                            return (
                                (1.0 - 4.0 * mixing_rate) * centre
                                + (coef[k, place, 0] * east + coef[k, place, 1] * west)
                                + (coef[k, place, 2] * north + coef[k, place, 3] * south)
                            )

                        new_main[x] = mixed(
                            0, m, main[x + 1], main[x - 1],
                            jnp.where(last_lane, e_down, m_down), jnp.where(first_lane, e_up, m_up),
                        )
                        if step < STEPS - 1:
                            new_side[x] = mixed(
                                1, e, side[x + 1], side[x - 1],
                                jnp.where(last_lane, m_down, e_down), jnp.where(first_lane, m_up, e_up),
                            )
                    main, side = new_main, new_side
                for x in range(cx):
                    gs[x, level, :] = main[x]
                return carry

            lax.fori_loop(0, groups, group, 0)
            g_copy(c).start()

        if first < 2:
            for k in range(len(EDGE_DIRS)):
                edge_copy(k, first).wait_recv()
        each_chunk(one, first, last)

    tall = cy
    base = lax.broadcasted_iota(jnp.int32, (tall, cap), 0)
    live_row = lax.broadcasted_iota(jnp.int32, (1, cap), 1)

    def owner_weights(q, carry):
        cols = pl.ds(pl.multiple_of(q * cap, cap), cap)
        live = live_row < counts_ref[0, 0, q]
        cell = [cells_ref[p, :, cols] for p in range(cells_ref.shape[0])]
        weight = [jnp.where(live, weights_ref[p, :, cols], 0.0) for p in range(cells_ref.shape[0])]

        def row_weights(x, inner):
            total = jnp.zeros((tall, cap), jnp.float32)
            for p in range(len(cell)):
                total = total + jnp.where(base == cell[p] - x * tall, weight[p], 0.0)
            high, low = halves(total)
            at = pl.ds(pl.multiple_of(x * tall, tall), tall)
            w_hi[at, cols] = high
            w_lo[at, cols] = low
            return inner

        lax.fori_loop(0, cx, row_weights, 0)
        return carry


    wide = 2 * cap if n_obs % 2 == 0 else cap

    def interpolate(pieces, keep):
        parts = [halves(v) for v in pieces]
        high = jnp.concatenate([p[0] for p in parts], axis=1)
        low = jnp.concatenate([p[1] for p in parts], axis=1)
        both = jnp.concatenate([high, low], axis=0)
        tall_in = high.shape[0]

        def one(b, carry):
            cols = pl.ds(pl.multiple_of(b * wide, wide), wide)
            main = dot(both, w_hi[:, cols])
            total = main[:tall_in] + (main[tall_in:] + dot(high, w_lo[:, cols]))
            for j in range(wide // cap):
                keep(b * (wide // cap) + j, total[:, j * cap : (j + 1) * cap])
            return carry

        lax.fori_loop(0, rows // wide, one, 0)

    def keep_pf(q, value):
        pf[q] = value

    def interpolate_forcing():
        lax.fori_loop(0, n_obs, owner_weights, 0)
        interpolate([f_ref[pl.ds(x, levels, stride=cx), :] for x in range(cx)], keep_pf)

    barrier = pltpu.get_barrier_semaphore()
    greeted = [neighbour(*d) for d in DIRS] + [peer(by) for by in range(1, n_obs)] + [along(1), along(-1)]
    for to in greeted:
        pl.semaphore_signal(barrier, inc=1, device_id=to, device_id_type=MESH)

    pairs = (
        (winds_in, winds_ref), (f_in, f_ref), (cells_in, cells_ref), (weights_in, weights_ref),
        (counts_in, counts_ref), (mixing_in, mixing_ref), (jac_in, jac_ref),
    )
    fetches = [pltpu.make_async_copy(src, dst, in_sem.at[i]) for i, (src, dst) in enumerate(pairs)]
    for fetch in fetches:
        fetch.start()
    for fetch in fetches:
        fetch.wait()

    @pl.when(slot == 0)
    def _():
        pack(f_ref)

    @pl.when(slot > 0)
    def _():
        interpolate_forcing()

    pl.semaphore_wait(barrier, len(greeted))

    @pl.when(slot < n_slot - 1)
    def _():
        for k in range(len(DIRS)):
            rate_copy(k).start()

    @pl.when(slot == 0)
    def _():
        send_halos()
        build_coefs()
        forward(0, 1)
        forward(1, chunks)
        interpolate_forcing()

    for by in range(1, n_obs):
        pf_copy(by).start()

    eye = jnp.where(
        lax.broadcasted_iota(jnp.int32, (levels, levels), 0) == lax.broadcasted_iota(jnp.int32, (levels, levels), 1),
        1.0, 0.0,
    )
    power = eye + mixing_ref[...]
    for _ in range(STEPS.bit_length() - 1):
        power = exact(power, power)
    jac = jac_ref[...]

    @pl.when(slot > 0)
    def _():
        table_hi[...], table_lo[...] = halves(jnp.concatenate([jac, exact(jac, power)], axis=1))

    @pl.when(slot > 0)
    def _():
        def one(c):
            g_copy(c).wait_recv()

            def keep_pg(q, value):
                pg[q, part(c), :] = value

            interpolate([gr[x, part(c), :] for x in range(cx)], keep_pg)
            for by in range(1, n_obs):
                pg_copy(by, c).start()

        each_chunk(one)
        power_parts = halves(power)

        for x in range(cx):
            state = dot3(power_parts, halves(gr[x])) + f_ref[pl.ds(x, levels, stride=cx), :]
            state_ref[pl.ds(x, levels, stride=cx), :] = state

    @pl.when(slot == 0)
    def _():
        state_ref[...] = f_ref[...]

    if n_slot > 2:
        @pl.when((slot > 0) & (slot < n_slot - 1))
        def _():
            pack(state_ref)
            send_halos()
            build_coefs()
            forward(0, 1)
            forward(1, chunks)

    def owner_out(o, value):
        rad_ref[:, pl.ds(pl.multiple_of(o * cap, cap), cap)] = value

    rf[obs] = pf[obs]
    for by in range(1, n_obs):
        pf_copy(by).wait_recv()

    @pl.when(slot > 0)
    def _():
        rg[obs] = pg[obs]

        def arrived(c):
            for by in range(1, n_obs):
                pg_copy(by, c).wait_recv()

        each_chunk(arrived)
        table = (table_hi[...], table_lo[...])

        def one(o, carry):
            owner_out(o, dot3(table, halves(jnp.concatenate([rf[o], rg[o]], axis=0))))
            return carry

        lax.fori_loop(0, n_obs, one, 0)

    @pl.when(slot == 0)
    def _():
        table = halves(jac)

        def one(o, carry):
            owner_out(o, dot3(table, halves(rf[o])))
            return carry

        lax.fori_loop(0, n_obs, one, 0)

    for by in range(1, n_obs):
        pf_copy(by).wait_send()

    @pl.when(slot > 0)
    def _():
        def left(c):
            for by in range(1, n_obs):
                pg_copy(by, c).wait_send()

        each_chunk(left)

    @pl.when(slot < n_slot - 1)
    def _():
        for k in range(len(DIRS)):
            rate_copy(k).wait_send()

        def left(c):
            for k in range(len(TILE_DIRS)):
                halo_copy(k, c).wait_send()
            g_copy(c).wait_send()

        each_chunk(left)
        for k in range(len(EDGE_DIRS)):
            for i in range(2):
                edge_copy(k, i).wait_send()


def write_out(states, radiances, states_out, radiances_out, sem):
    copies = [
        pltpu.make_async_copy(states, states_out, sem.at[0]),
        pltpu.make_async_copy(radiances, radiances_out, sem.at[1]),
    ]
    for copy in copies:
        copy.start()
    for copy in copies:
        copy.wait()


def solution(mesh):
    n_slot, n_tile, n_obs = (mesh.shape[a] for a in ("slot", "tile", "obs"))

    def local(forcing, winds, mixing, observation_columns, obs_weights, obs_counts, jacobian):
        _, levels, cx, cy = forcing.shape
        rows = observation_columns.shape[2]
        cap = rows // n_obs
        channels = jacobian.shape[2]
        chunks = levels // (SUB * (LANES // (cx * 2 * STEPS)))
        f32, bf16 = jnp.float32, jnp.bfloat16
        dma = pltpu.SemaphoreType.DMA
        vmem = pl.BlockSpec(memory_space=pltpu.VMEM)
        hbm = pl.BlockSpec(memory_space=pltpu.HBM)
        states, radiances = pl.pallas_call(
            functools.partial(kernel, n_slot, n_tile, n_obs),
            out_shape=(
                jax.ShapeDtypeStruct((levels * cx, cy), f32),
                jax.ShapeDtypeStruct((channels, rows), f32),
            ),
            in_specs=[hbm] * 7,
            out_specs=(vmem, vmem),
            scratch_shapes=[
                pltpu.VMEM((levels * cx, cy), f32),
                pltpu.VMEM((2, cx, cy), f32),
                pltpu.VMEM(mixing.shape, f32),
                pltpu.VMEM(observation_columns.shape, jnp.int32),
                pltpu.VMEM(obs_weights.shape, f32),
                pltpu.SMEM(obs_counts.shape, jnp.int32),
                pltpu.VMEM((channels, levels), f32),
                dma((7,)),
                pltpu.VMEM((channels, 2 * levels), bf16),
                pltpu.VMEM((channels, 2 * levels), bf16),
                pltpu.VMEM((cx, levels, cy), f32),
                pltpu.VMEM((2, STEPS, levels, cy), f32),
                pltpu.VMEM((chunks, SUB, LANES), f32),
                pltpu.VMEM((len(EDGE_DIRS), chunks, SUB, LANES), f32),
                pltpu.VMEM((len(DIRS), 2, cx, cy), f32),
                pltpu.VMEM((cx + 2 * STEPS, 2, 4, SUB, LANES), f32),
                pltpu.VMEM((cx, levels, cy), f32),
                pltpu.VMEM((cx, levels, cy), f32),
                pltpu.VMEM((cx * cy, rows), bf16),
                pltpu.VMEM((cx * cy, rows), bf16),
                pltpu.VMEM((n_obs, levels, cap), f32),
                pltpu.VMEM((n_obs, levels, cap), f32),
                pltpu.VMEM((n_obs, levels, cap), f32),
                pltpu.VMEM((n_obs, levels, cap), f32),
                dma((2, chunks)), dma((2, chunks)),
                dma((len(EDGE_DIRS), 2)), dma((len(EDGE_DIRS), 2)),
                dma((len(DIRS),)), dma((len(DIRS),)),
                dma((chunks,)), dma((chunks,)),
                dma((n_obs,)), dma((n_obs,)),
                dma((n_obs, chunks)), dma((n_obs, chunks)),
            ],
            compiler_params=pltpu.CompilerParams(
                collective_id=0, has_side_effects=True, vmem_limit_bytes=48 * 1024 * 1024
            ),
        )(*(pltpu.with_memory_space_constraint(v, pltpu.HBM) for v in (
            forcing.reshape(levels * cx, cy),
            winds.reshape(2, cx, cy),
            mixing,
            observation_columns,
            obs_weights,
            obs_counts,
            jacobian.reshape(channels, levels),
        )))
        states, radiances = pl.pallas_call(
            write_out,
            out_shape=(
                jax.ShapeDtypeStruct((levels * cx, cy), f32),
                jax.ShapeDtypeStruct((channels, rows), f32),
            ),
            in_specs=[vmem, vmem],
            out_specs=(hbm, hbm),
            scratch_shapes=[dma((2,))],
            compiler_params=pltpu.CompilerParams(vmem_limit_bytes=2 * 1024 * 1024),
        )(states, radiances)
        return states.reshape(1, levels, cx, cy), radiances.reshape(1, channels, rows)

    return jax.shard_map(
        local,
        mesh=mesh,
        in_specs=(
            P("slot", None, "tile", "obs"),
            P(None, "slot", "tile", "obs"),
            P(),
            P(None, "slot", ("tile", "obs")),
            P(None, "slot", ("tile", "obs")),
            P("slot", ("tile", "obs"), None),
            P("slot", "obs", None, None),
        ),
        out_specs=(P("slot", None, "tile", "obs"), P("slot", None, ("tile", "obs"))),
        check_vma=False,
    )
```
